32 devices in a mesh: rows: 4 (over y, core), cols: 8 (over z, x).
Axes of the slice: x: 2, y: 2, z: 4, core: 2. Of those that a mesh axis runs over, the one named last changes fastest.
Arguments:
- features: bfloat16 [32768, 2048], P(('rows', 'cols')), may hold values from -6 to 6
- w_in: bfloat16 [2048, 1024], replicated, may hold values from -0.125 to 0.125
- w_out: bfloat16 [1024, 256], replicated, may hold values from -0.1875 to 0.1875
- item_ids: int32 [32768], P(('rows', 'cols')), may hold values from 0 to 32767, as said below
- item_counts: int32 [32768], P(('rows', 'cols')), may hold values from 0 to 65535
- owners: int32 [32768, 1], P(('rows', 'cols')), may hold values from 0 to 31; in each aligned block of 1024 rows (0 to 1023, 1024 to 2047, ...) at most 64 rows name the same one
- queries: bfloat16 [8192, 256], P('rows'), may hold values from -60 to 60
- positives: int32 [8192], replicated, may hold values from 0 to 32767, as said below
Outputs:
- cache_emb: bfloat16 [65536, 256], P(('rows', 'cols'))
- cache_ids: int32 [65536], P(('rows', 'cols'))
- query_loss: float32 [8192], P('rows')
The draws below stay inside these ranges and needn't reach their ends.
Inputs may be any that keep to these rules, and one draw needn't show every extreme that they name: `item_ids`: all ids are different. `owners`: the items of one device name each owner at most 64 times; some owner is named exactly 64 times by one device's items. `positives`: each is the id of some item.
All inputs are finite; a program needn't handle non-finite values.
Results may differ from the reference program's by a relative error of at most 0.0049.
Values may be sent and summed in bfloat16 or wider, within the bound.
A program may use at most 128 MiB of HBM per device.

```python
import math
import jax
import jax.numpy as jnp
import numpy as np
from jax import lax

F_IN = 2048
HID = 1024
EMB = 256
ITEMS_DEV = 1024
ITEMS = 32768
CAP = 64
QUERIES = 8192
POOL = 65536
DEVICES = 32


def shared_ids(key):
    return jax.random.permutation(jax.random.fold_in(key, 29), ITEMS).astype(jnp.int32)


def draw_item_ids(key, part):
    return shared_ids(key)


def draw_positives(key, part):
    identity = shared_ids(key)
    key_order, key_offset = jax.random.split(jax.random.fold_in(key, 31), 2)
    blocks = QUERIES // DEVICES
    scores = jax.random.randint(key_order, (blocks, DEVICES), 0, 1 << 20) * DEVICES + jnp.arange(DEVICES, dtype=jnp.int32)[None, :]
    producer = jnp.argsort(scores, axis=1, stable=True).astype(jnp.int32).reshape(QUERIES)
    offset = jax.random.randint(key_offset, (QUERIES,), 0, ITEMS_DEV).astype(jnp.int32)
    return identity[producer * ITEMS_DEV + offset].astype(jnp.int32)


def draw_queries(key, part):
    key_base = jax.random.fold_in(jax.random.fold_in(key, 17), 0)
    values = jax.random.normal(key_base, (QUERIES, EMB), jnp.float32)
    return jnp.clip(values, -6.0, 6.0).astype(jnp.bfloat16)


def place_ends(drawn, stream_key, low, top_value):
    shape = drawn.shape
    place = [jax.random.randint(jax.random.fold_in(stream_key, axis), (), 0, shape[axis]) for axis in range(len(shape))]
    drawn = drawn.at[tuple(place)].set(low)
    longest = shape.index(max(shape))
    place[longest] = (place[longest] + 1) % shape[longest]
    return drawn.at[tuple(place)].set(top_value)


def block_levels(key, dims, pieces, smallest, largest):
    gain = 1.0
    for position, parts in pieces:
        draws = jax.random.uniform(jax.random.fold_in(jax.random.fold_in(key, 6), position), (parts,), jnp.float32, smallest / len(pieces), largest / len(pieces))
        gain = gain * jnp.repeat(jnp.exp(draws), dims[position] // parts).reshape((-1,) + (1,) * (len(dims) - 1 - position))
    return gain


def rank_table(count, slope):
    portions = [(1 << 20) // math.isqrt(standing ** slope) + 1 for standing in range(1, count + 1)]
    deviation = 1 + sum(portions) // (1 << 30)
    return np.cumsum(np.array([max(1, weight // deviation) for weight in portions]))


def ranked(stream_key, dims, count, skew):
    table = rank_table(count, skew)
    lot = jax.random.randint(jax.random.fold_in(stream_key, 1), dims, 0, int(table[count - 1]))
    rank = jnp.searchsorted(jnp.asarray(table, jnp.int32), lot, side="right")
    return jax.random.permutation(jax.random.fold_in(stream_key, 2), count)[rank].astype(jnp.int32)


def assign_block(rng, own, number, rows, amount, top, most, slope):
    order = jax.random.permutation(rng, amount)
    packed, common = shares(amount, rows * top, most, slope, True), shares(amount, rows * top, most, slope, False)
    places = jnp.arange(amount)

    def named(tallies, rotation):
        used = int((tallies > 0).sum())
        fixed = max(1, used // 4)
        passed = fixed + (places - fixed + rotation * (used - fixed)) % max(1, amount - fixed)
        return jnp.zeros((amount,), jnp.int32).at[order[jnp.where(places < fixed, places, passed)]].set(jnp.asarray(tallies, jnp.int32))

    tallies = jnp.where(number % 4 == 0, named(packed, number // 4), named(common, number - number // 4 - 1))
    mixed = jax.random.permutation(jax.random.fold_in(own, 3), amount)
    source_of, taker = mixed[0:amount // 2 * 2:2], mixed[1:amount // 2 * 2:2]
    room = jnp.minimum(tallies[source_of] - 1, most - tallies[taker]) // 2
    room = jnp.where((source_of == order[0]) | (taker == order[0]) | (tallies[taker] == 0), 0, jnp.maximum(room, 0))
    passed = jax.random.randint(jax.random.fold_in(own, 4), (amount // 2,), 0, 1 << 20) % (room + 1)
    tallies = tallies.at[source_of].add(-passed).at[taker].add(passed)
    items = jnp.searchsorted(jnp.cumsum(tallies), jnp.arange(rows * top), side="right").astype(jnp.int32)
    listing = items.reshape(top, rows).T
    listing = listing[jax.random.permutation(jax.random.fold_in(own, 1), rows)]
    rotation = jax.random.randint(jax.random.fold_in(own, 2), (rows, 1), 0, top)
    return jnp.take_along_axis(listing, (jnp.arange(top)[None, :] + rotation) % top, axis=1)


def shares(number_of, total, most, skew, full):
    loads = [(1 << 20) // math.isqrt(rank ** skew) + 1 for rank in range(1, number_of + 1)]
    largest = most if full else min(most, max(-(-total // number_of), total * loads[0] // sum(loads)))
    least = 1 if total - largest >= number_of - 1 else 0
    given, spare = [largest] + [least] * (number_of - 1), total - largest - least * (number_of - 1)
    while spare > 0:
        movable = [i for i in range(1, number_of) if given[i] < largest] or [i for i in range(1, number_of) if given[i] < most]
        pool, left = sum([loads[i] for i in movable]), spare
        for i in movable:
            more = min(most - given[i], max(1, left * loads[i] // pool), spare)
            given[i] = given[i] + more
            spare = spare - more
    return np.array(given)


def normal_values(stream_key, extent, spread, reach, cuts=(), held_as=jnp.bfloat16):
    entries = jax.random.normal(stream_key, extent, jnp.float32) * spread
    if len(cuts) > 0:
        entries = block_levels(stream_key, extent, cuts, -0.22, 0.18) * entries
    return jnp.clip(entries, min=-reach, max=reach).astype(held_as)


def setup_inputs(seed: int = 0) -> dict:
    key_of = jax.random.split(jax.random.key(seed), 9)
    features = normal_values(key_of[0], (ITEMS, F_IN), 1.0, 6.0, ((0, 32),))
    w_in = normal_values(key_of[1], (F_IN, HID), F_IN ** -0.5, 0.125)
    w_out = normal_values(key_of[2], (HID, EMB), HID ** -0.5, 0.1875)
    item_ids = draw_item_ids(jax.random.fold_in(key_of[8], 71), 0)
    item_counts = place_ends(ranked(key_of[4], (ITEMS,), 65536, 2), jax.random.fold_in(key_of[4], 3), 0, 65535).astype(jnp.int32)
    owners_keys = jax.random.split(jax.random.fold_in(key_of[5], 1), ITEMS // ITEMS_DEV)
    owners_turns = jax.random.permutation(jax.random.fold_in(key_of[5], 3), ITEMS // ITEMS_DEV)
    owners = jax.vmap(lambda own, number: assign_block(jax.random.fold_in(key_of[5], 2), own, number, ITEMS_DEV, DEVICES, 1, CAP, 1))(owners_keys, owners_turns).reshape((ITEMS, 1))
    queries = draw_queries(jax.random.fold_in(key_of[8], 71), 0)
    positives = draw_positives(jax.random.fold_in(key_of[8], 71), 0)
    return dict(features=features, w_in=w_in, w_out=w_out, item_ids=item_ids, item_counts=item_counts, owners=owners, queries=queries, positives=positives)


def item_tower(block_rows, w_in, w_out):
    hidden = jnp.maximum(jnp.dot(block_rows, w_in, preferred_element_type=jnp.float32), 0.0).astype(jnp.bfloat16)
    return jnp.dot(hidden, w_out, preferred_element_type=jnp.float32).astype(jnp.bfloat16)

def rank_rows(owner_row):
    onehot = (owner_row[:, None] == jnp.arange(DEVICES, dtype=jnp.int32)[None, :]).astype(jnp.int32)
    before = jnp.cumsum(onehot, axis=0) - onehot
    return lax.optimization_barrier(jnp.sum(before * onehot, axis=1)).astype(jnp.int32)

def reference(features, w_in, w_out, item_ids, item_counts, owners, queries, positives):

    def tower_block(block_rows):
        return item_tower(block_rows, w_in, w_out)
    embedded = lax.map(tower_block, features.reshape(DEVICES, ITEMS_DEV, F_IN)).reshape(ITEMS, EMB)
    owner_index = owners[:, 0].astype(jnp.int32)
    rank_within = lax.map(rank_rows, owner_index.reshape(DEVICES, ITEMS_DEV)).reshape(ITEMS)
    source = jnp.arange(ITEMS, dtype=jnp.int32) // ITEMS_DEV
    cache_index = (owner_index * (DEVICES * CAP) + source * CAP + rank_within).astype(jnp.int32)
    cache_emb = jnp.zeros((POOL, EMB), jnp.bfloat16).at[cache_index].set(embedded)
    cache_ids = jnp.full((POOL,), -1, jnp.int32).at[cache_index].set(item_ids)
    log_q = jnp.log1p(item_counts.astype(jnp.float32))
    score_scale = 4.0 / math.sqrt(EMB)
    row_of_id = jnp.zeros((ITEMS,), jnp.int32).at[item_ids.astype(jnp.int32)].set(jnp.arange(ITEMS, dtype=jnp.int32))
    pos_row = row_of_id[positives.astype(jnp.int32)].astype(jnp.int32)
    pos_emb = embedded[pos_row]
    pos_logit = lax.optimization_barrier(jnp.sum(queries.astype(jnp.float32) * pos_emb.astype(jnp.float32), axis=1)) * score_scale - log_q[pos_row]
    block_rows = min(QUERIES, 512)
    key_rows = embedded.T

    def block_lse(query_block):
        raw_scores = jnp.dot(query_block, key_rows, preferred_element_type=jnp.float32) * score_scale - log_q[None, :]
        highest = lax.optimization_barrier(jnp.max(raw_scores, axis=1, keepdims=True))
        return highest[:, 0] + jnp.log(lax.optimization_barrier(jnp.sum(jnp.exp(raw_scores - highest), axis=1)))
    log_total = lax.map(block_lse, queries.reshape(QUERIES // block_rows, block_rows, EMB)).reshape(QUERIES)
    query_loss = log_total - pos_logit
    return (cache_emb, cache_ids, query_loss)
```

```python
import functools
import math

import jax
import jax.numpy as jnp
from jax import lax
from jax.experimental import pallas as pl
from jax.experimental.pallas import tpu as pltpu
from jax.sharding import PartitionSpec as P

MESH = pl.DeviceIdType.MESH
LANES = 128
LOW = -3.0e38
NT = (((1,), (1,)), ((), ()))


def kernel(
    n_rows, n_cols, cap, chunks, key_tile, query_tile,
    feat_hbm, w_in_hbm, w_out_hbm, ids_ref, counts_ref, owners_ref, q_hbm, pos_ref,
    cache_ref, cids_ref, loss_ref,
    feat, w_in, w_out, q, onehot, emb, aux, keyid, keylq, send, idsend, idrecv, pos,
    stats, parts, picked,
    load_sem, feat_sem, own_sem, aux_send, aux_recv, id_send, id_recv,
    emb_send, emb_recv, fwd_send, fwd_recv, a2a_send, a2a_recv, stat_send, stat_recv,
):
    n_dev = n_rows * n_cols
    n_y = n_rows // 2
    items, width = emb.shape[1] * emb.shape[2], emb.shape[3]
    chunk = items // chunks
    q_dev = q.shape[0]
    slots = n_dev * cap
    pack = LANES // cap
    row, col = lax.axis_index("rows"), lax.axis_index("cols")
    me = row * n_cols + col
    sib = row + 1 - 2 * lax.rem(row, 2)

    def place(index):
        return (lax.div(index, n_cols), lax.rem(index, n_cols))

    loads = [
        pltpu.make_async_copy(w_in_hbm, w_in, load_sem.at[0]),
        pltpu.make_async_copy(w_out_hbm, w_out, load_sem.at[1]),
        pltpu.make_async_copy(q_hbm, q, load_sem.at[2]),
    ]

    def feat_copy(i):
        return pltpu.make_async_copy(feat_hbm.at[i], feat.at[i], feat_sem.at[i])

    loads[0].start()
    feat_copy(0).start()
    loads[1].start()
    for i in range(1, chunks):
        feat_copy(i).start()
    loads[2].start()

    barrier = pltpu.get_barrier_semaphore()

    @pl.loop(1, n_dev)
    def _(k):
        pl.semaphore_signal(
            barrier, inc=1, device_id=place(lax.rem(me + k, n_dev)), device_id_type=MESH
        )

    aux[0] = jnp.zeros_like(aux[0])
    for i in range(items // LANES):
        lanes = slice(i * LANES, (i + 1) * LANES)
        aux[0, 0:1, lanes] = ids_ref[i : i + 1, :]
        aux[0, 1:2, lanes] = counts_ref[i : i + 1, :]
        aux[0, 2:3, lanes] = owners_ref[i : i + 1, :]
    for i in range(q_dev // LANES):
        pos[0:1, i * LANES : (i + 1) * LANES] = pos_ref[pl.ds(row * (q_dev // LANES) + i, 1), :]

    owner = aux[0, 2:3, :]
    named = (lax.broadcasted_iota(jnp.int32, (n_dev, items), 0) == owner).astype(jnp.float32)
    earlier = (
        lax.broadcasted_iota(jnp.int32, (items, items), 0)
        < lax.broadcasted_iota(jnp.int32, (items, items), 1)
    ).astype(jnp.float32).astype(jnp.bfloat16)
    before = jnp.dot(named.astype(jnp.bfloat16), earlier, preferred_element_type=jnp.float32)
    rank = jnp.sum(before * named, axis=0, keepdims=True).astype(jnp.int32)
    slot = owner * cap + rank

    value = aux[0, 0:1, :] + 1
    line = lax.broadcasted_iota(jnp.int32, (16, items), 0)
    digits = jnp.zeros((16, items), jnp.float32)
    for j in range(4):
        digit = lax.rem(lax.div(value, 256**j), 256).astype(jnp.float32)
        digits = jnp.where(line == j, digit, digits)
    digits = digits.astype(jnp.bfloat16)
    piece = onehot.shape[1]
    weight_line = lax.broadcasted_iota(jnp.int32, (16, piece), 0)
    weight = jnp.where(
        weight_line == 0, 1, jnp.where(weight_line == 1, 256, jnp.where(weight_line == 2, 65536, 0))
    ) + jnp.where(weight_line == 3, 1 << 24, 0)

    @pl.loop(0, slots // piece)
    def _(g):
        hot = (
            lax.broadcasted_iota(jnp.int32, (piece, items), 0) + g * piece == slot
        ).astype(jnp.float32).astype(jnp.bfloat16)
        onehot[g] = hot
        found = lax.dot_general(digits, hot, NT, preferred_element_type=jnp.float32)
        joined = jnp.sum(found.astype(jnp.int32) * weight, axis=0, keepdims=True) - 1
        for i in range(piece // LANES):
            idsend[g * (piece // LANES) + i] = jnp.broadcast_to(
                joined[:, i * LANES : (i + 1) * LANES], (8, LANES)
            )

    def spread(s):
        ids_row = aux[s, 0:1, :]
        lq_row = jnp.log(1.0 + aux[s, 1:2, :].astype(jnp.float32)) * (math.sqrt(width) / 4.0)
        for i in range(items // LANES):
            lanes = slice(i * LANES, (i + 1) * LANES)
            keyid[lanes, :] = jnp.broadcast_to(ids_row[:, lanes], (LANES, LANES)).T
            keylq[lanes, :] = jnp.broadcast_to(lq_row[:, lanes], (LANES, LANES)).T

    stats[0:1, :] = jnp.full((1, q_dev), LOW, jnp.float32)
    stats[1:3, :] = jnp.zeros((2, q_dev), jnp.float32)

    pl.semaphore_wait(barrier, n_dev - 1)

    def y_row(base, j):
        return lax.rem(base + n_rows - 2 * j, n_rows)

    aux_copies = []
    for s in range(1, n_rows):
        target = y_row(sib if s % 2 else row, s // 2)
        aux_copies.append(
            pltpu.make_async_remote_copy(
                src_ref=aux.at[0], dst_ref=aux.at[s], send_sem=aux_send.at[s],
                recv_sem=aux_recv.at[s], device_id=(target, col), device_id_type=MESH,
            )
        )
    for copy in aux_copies:
        copy.start()

    def id_copy(k):
        to = lax.rem(me + k, n_dev)
        return pltpu.make_async_remote_copy(
            src_ref=idsend.at[lax.div(to, pack)],
            dst_ref=idrecv.at[lax.div(me, pack), lax.rem(me, pack)],
            send_sem=id_send.at[k], recv_sem=id_recv.at[k],
            device_id=place(to), device_id_type=MESH,
        )

    @pl.loop(1, n_dev)
    def _(k):
        id_copy(k).start()

    def own_emb_copy(s, i):
        target = sib if s == 1 else y_row(row, s // 2)
        return pltpu.make_async_remote_copy(
            src_ref=emb.at[0, i], dst_ref=emb.at[s, i], send_sem=emb_send.at[s, i],
            recv_sem=emb_recv.at[s, i], device_id=(target, col), device_id_type=MESH,
        )

    def fwd_copy(s, i):
        return pltpu.make_async_remote_copy(
            src_ref=emb.at[s, i], dst_ref=emb.at[s + 1, i], send_sem=fwd_send.at[s, i],
            recv_sem=fwd_recv.at[s, i], device_id=(sib, col), device_id_type=MESH,
        )

    direct = [1] + [2 * j for j in range(1, n_y)]
    loads[0].wait()
    loads[1].wait()

    @pl.loop(0, chunks)
    def _(i):
        feat_copy(i).wait()
        hidden = jnp.maximum(
            jnp.dot(feat[i], w_in[...], preferred_element_type=jnp.float32), 0.0
        ).astype(jnp.bfloat16)
        emb[0, i] = jnp.dot(hidden, w_out[...], preferred_element_type=jnp.float32).astype(
            jnp.bfloat16
        )
        for s in reversed(direct):
            own_emb_copy(s, i).start()

    each = piece // cap

    @pl.loop(0, slots // piece)
    def _(g):
        total = jnp.zeros((piece, width), jnp.float32)
        for i in range(chunks):
            total = total + jnp.dot(
                onehot[g, :, i * chunk : (i + 1) * chunk], emb[0, i],
                preferred_element_type=jnp.float32,
            )
        rows_out = total.astype(jnp.bfloat16)
        for t in range(each):
            send[g * each + t] = rows_out[t * cap : (t + 1) * cap, :]

    def a2a_copy(k):
        to = lax.rem(me + k, n_dev)
        return pltpu.make_async_remote_copy(
            src_ref=send.at[to], dst_ref=cache_ref.at[me],
            send_sem=a2a_send.at[k], recv_sem=a2a_recv.at[k],
            device_id=place(to), device_id_type=MESH,
        )

    own_block = pltpu.make_async_copy(send.at[me], cache_ref.at[me], own_sem)

    @pl.loop(1, n_dev)
    def _(k):
        a2a_copy(k).start()

    own_block.start()
    loads[2].wait()

    steep = 4.0 / math.sqrt(width) * math.log2(math.e)

    def score(s, i):
        @pl.loop(0, chunk // key_tile)
        def _(t):
            base = i * chunk + t * key_tile
            keys = emb[s, i, pl.ds(t * key_tile, key_tile), :]
            wide = query_tile // LANES
            ident = jnp.concatenate([keyid[pl.ds(base, key_tile), :]] * wide, axis=1)
            lq = jnp.concatenate([keylq[pl.ds(base, key_tile), :]] * wide, axis=1)
            for u in range(q_dev // query_tile):
                lanes = slice(u * query_tile, (u + 1) * query_tile)
                raw = lax.dot_general(keys, q[lanes, :], NT, preferred_element_type=jnp.float32) - lq
                hit = jnp.sum(jnp.where(ident == pos[:, lanes], raw, 0.0), axis=0, keepdims=True)
                old = stats[0:1, lanes]
                top = jnp.maximum(old, jnp.max(raw, axis=0, keepdims=True))
                total = jnp.sum(jnp.exp2((raw - top) * steep), axis=0, keepdims=True)
                stats[0:1, lanes] = top
                stats[1:2, lanes] = stats[1:2, lanes] * jnp.exp2((old - top) * steep) + total
                stats[2:3, lanes] = stats[2:3, lanes] + hit

    spread(0)

    @pl.loop(0, chunks)
    def _(i):
        score(0, i)

    for s in range(1, n_rows):
        aux_copies[s - 1].wait()
        spread(s)

        @pl.loop(0, chunks)
        def _(i, s=s):
            if s == 1:
                own_emb_copy(1, i).wait()
            elif s % 2 == 0:
                own_emb_copy(s, i).wait()
                fwd_copy(s, i).start()
            else:
                fwd_copy(s - 1, i).wait()
            score(s, i)

    scale = 4.0 / math.sqrt(width)
    parts[0, 0:1, :] = stats[0:1, :] * scale + jnp.log(stats[1:2, :])
    parts[0, 1:2, :] = stats[2:3, :] * scale

    def stat_copy(k):
        return pltpu.make_async_remote_copy(
            src_ref=parts.at[0], dst_ref=parts.at[k],
            send_sem=stat_send.at[k], recv_sem=stat_recv.at[k],
            device_id=(row, lax.rem(col + k, n_cols)), device_id_type=MESH,
        )

    @pl.loop(1, n_cols)
    def _(k):
        stat_copy(k).start()

    idrecv[lax.div(me, pack), lax.rem(me, pack)] = idsend[lax.div(me, pack)]

    @pl.loop(1, n_dev)
    def _(k):
        id_copy(k).wait()

    lane = lax.broadcasted_iota(jnp.int32, (n_dev // pack, LANES), 1)
    result = jnp.zeros((n_dev // pack, LANES), jnp.int32)
    for j in range(pack):
        shift = lax.rem(j + pack - lax.rem(me, pack), pack) * cap
        for g in range(n_dev // pack):
            picked[g : g + 1, :] = idrecv[g, j, 0:1, :]
        turned = pltpu.roll(picked[...], shift, 1)
        result = jnp.where(lax.div(lane, cap) == j, turned, result)
    cids_ref[...] = result

    @pl.loop(1, n_cols)
    def _(k):
        stat_copy(k).wait()

    highest = parts[0, 0:1, :]
    for k in range(1, n_cols):
        highest = jnp.maximum(highest, parts[k, 0:1, :])
    summed = jnp.zeros_like(highest)
    positive = jnp.zeros_like(highest)
    for k in range(n_cols):
        summed = summed + jnp.exp(parts[k, 0:1, :] - highest)
        positive = positive + parts[k, 1:2, :]
    loss = highest + jnp.log(summed) - positive
    for i in range(q_dev // LANES):
        loss_ref[i : i + 1, :] = loss[:, i * LANES : (i + 1) * LANES]

    @pl.loop(1, n_dev)
    def _(k):
        a2a_copy(k).wait()

    own_block.wait()


def local(n_rows, n_cols, features, w_in, w_out, item_ids, item_counts, owners, queries, positives):
    n_dev = n_rows * n_cols
    items, wide = features.shape
    hid, width = w_out.shape
    cap = 2 * items // n_dev
    slots = n_dev * cap
    pack = LANES // cap
    q_dev = queries.shape[0]
    chunks = 4
    piece = 256
    bf16, i32, f32 = jnp.bfloat16, jnp.int32, jnp.float32
    hbm = pl.BlockSpec(memory_space=pl.ANY)
    vmem = pl.BlockSpec(memory_space=pltpu.VMEM)
    dma = pltpu.SemaphoreType.DMA
    cache, ids, loss = pl.pallas_call(
        functools.partial(kernel, n_rows, n_cols, cap, chunks, 256, 512),
        out_shape=(
            jax.ShapeDtypeStruct((n_dev, cap, width), bf16),
            jax.ShapeDtypeStruct((slots // LANES, LANES), i32),
            jax.ShapeDtypeStruct((q_dev // LANES, LANES), f32),
        ),
        in_specs=[hbm, hbm, hbm, vmem, vmem, vmem, hbm, vmem],
        out_specs=(hbm, vmem, vmem),
        scratch_shapes=[
            pltpu.VMEM((chunks, items // chunks, wide), bf16),
            pltpu.VMEM(w_in.shape, bf16),
            pltpu.VMEM(w_out.shape, bf16),
            pltpu.VMEM(queries.shape, bf16),
            pltpu.VMEM((slots // piece, piece, items), bf16),
            pltpu.VMEM((n_rows, chunks, items // chunks, width), bf16),
            pltpu.VMEM((n_rows, 8, items), i32),
            pltpu.VMEM((items, LANES), i32),
            pltpu.VMEM((items, LANES), f32),
            pltpu.VMEM((n_dev, cap, width), bf16),
            pltpu.VMEM((slots // LANES, 8, LANES), i32),
            pltpu.VMEM((n_dev // pack, pack, 8, LANES), i32),
            pltpu.VMEM((1, q_dev), i32),
            pltpu.VMEM((8, q_dev), f32),
            pltpu.VMEM((n_cols, 2, q_dev), f32),
            pltpu.VMEM((n_dev // pack, LANES), i32),
            dma((3,)), dma((chunks,)), dma,
            dma((n_rows,)), dma((n_rows,)),
            dma((n_dev,)), dma((n_dev,)),
            dma((n_rows, chunks)), dma((n_rows, chunks)),
            dma((n_rows, chunks)), dma((n_rows, chunks)),
            dma((n_dev,)), dma((n_dev,)),
            dma((n_cols,)), dma((n_cols,)),
        ],
        compiler_params=pltpu.CompilerParams(
            collective_id=0, has_side_effects=True, vmem_limit_bytes=56 * 1024 * 1024
        ),
        name="refresh",
    )(
        features.reshape(chunks, items // chunks, wide),
        w_in,
        w_out,
        item_ids.reshape(items // LANES, LANES),
        item_counts.reshape(items // LANES, LANES),
        owners.reshape(items // LANES, LANES),
        queries,
        positives.reshape(positives.shape[0] // LANES, LANES),
    )
    return cache.reshape(slots, width), ids.reshape(slots), loss.reshape(q_dev)


def solution(mesh):
    placed = (
        P(("rows", "cols"), None),
        P(),
        P(),
        P(("rows", "cols")),
        P(("rows", "cols")),
        P(("rows", "cols"), None),
        P("rows", None),
        P(),
    )
    return jax.shard_map(
        functools.partial(local, mesh.shape["rows"], mesh.shape["cols"]),
        mesh=mesh,
        in_specs=placed,
        out_specs=(P(("rows", "cols"), None), P(("rows", "cols")), P("rows")),
        check_vma=False,
    )
```

```python
import functools
import math

import jax
import jax.numpy as jnp
from jax import lax
from jax.experimental import pallas as pl
from jax.experimental.pallas import tpu as pltpu
from jax.sharding import PartitionSpec as P

MESH = pl.DeviceIdType.MESH
LANES = 128
LOW = -3.0e38
NT = (((1,), (1,)), ((), ()))


def kernel(
    n_rows, n_cols, cap, chunks, piece, key_tile, query_tile,
    feat_hbm, w_in_hbm, w_out_hbm, ids_ref, counts_ref, owners_ref, q_hbm, pos_ref,
    cache_ref, cids_ref, loss_ref,
    feat, w_in, w_out, q, emb, aux, keyid, keylq, send, idsend, idrecv, pos,
    stats, parts, picked,
    load_sem, feat_sem, own_sem, aux_send, aux_recv, id_send, id_recv,
    emb_send, emb_recv, fwd_send, fwd_recv, a2a_send, a2a_recv, stat_send, stat_recv,
):
    n_dev = n_rows * n_cols
    n_y = n_rows // 2
    items, width = emb.shape[1] * emb.shape[2], emb.shape[3]
    chunk = items // chunks
    q_dev = q.shape[0]
    slots = n_dev * cap
    pack = LANES // cap
    row, col = lax.axis_index("rows"), lax.axis_index("cols")
    me = row * n_cols + col
    sib = row + 1 - 2 * lax.rem(row, 2)

    def place(index):
        return (lax.div(index, n_cols), lax.rem(index, n_cols))

    loads = [
        pltpu.make_async_copy(w_in_hbm, w_in, load_sem.at[0]),
        pltpu.make_async_copy(w_out_hbm, w_out, load_sem.at[1]),
        pltpu.make_async_copy(q_hbm, q, load_sem.at[2]),
    ]

    def feat_copy(i):
        return pltpu.make_async_copy(feat_hbm.at[i], feat.at[i], feat_sem.at[i])

    loads[0].start()
    feat_copy(0).start()
    loads[1].start()
    for i in range(1, chunks):
        feat_copy(i).start()
    loads[2].start()

    barrier = pltpu.get_barrier_semaphore()

    @pl.loop(1, n_dev)
    def _(k):
        pl.semaphore_signal(
            barrier, inc=1, device_id=place(lax.rem(me + k, n_dev)), device_id_type=MESH
        )

    aux[0] = jnp.zeros_like(aux[0])
    for i in range(items // LANES):
        lanes = slice(i * LANES, (i + 1) * LANES)
        aux[0, 0:1, lanes] = ids_ref[i : i + 1, :]
        aux[0, 1:2, lanes] = counts_ref[i : i + 1, :]
        aux[0, 2:3, lanes] = owners_ref[i : i + 1, :]
    for i in range(q_dev // LANES):
        pos[:, i * LANES : (i + 1) * LANES] = jnp.broadcast_to(
            pos_ref[pl.ds(row * (q_dev // LANES) + i, 1), :], (8, LANES)
        )

    owner = aux[0, 2:3, :]
    named = (lax.broadcasted_iota(jnp.int32, (n_dev, items), 0) == owner).astype(jnp.float32)
    earlier = (
        lax.broadcasted_iota(jnp.int32, (items, items), 0)
        < lax.broadcasted_iota(jnp.int32, (items, items), 1)
    ).astype(jnp.float32).astype(jnp.bfloat16)
    before = jnp.dot(named.astype(jnp.bfloat16), earlier, preferred_element_type=jnp.float32)
    rank = jnp.sum(before * named, axis=0, keepdims=True).astype(jnp.int32)
    slot = owner * cap + rank

    value = aux[0, 0:1, :] + 1
    line = lax.broadcasted_iota(jnp.int32, (16, items), 0)
    digits = jnp.zeros((16, items), jnp.float32)
    for j in range(4):
        digit = lax.rem(lax.div(value, 256**j), 256).astype(jnp.float32)
        digits = jnp.where(line == j, digit, digits)
    digits = digits.astype(jnp.bfloat16)
    weight_line = lax.broadcasted_iota(jnp.int32, (16, piece), 0)
    weight = jnp.where(
        weight_line == 0, 1, jnp.where(weight_line == 1, 256, jnp.where(weight_line == 2, 65536, 0))
    ) + jnp.where(weight_line == 3, 1 << 24, 0)

    def spread(s):
        ids_row = aux[s, 0:1, :]
        lq_row = jnp.log(1.0 + aux[s, 1:2, :].astype(jnp.float32)) * (math.sqrt(width) / 4.0)
        for i in range(items // LANES):
            lanes = slice(i * LANES, (i + 1) * LANES)
            keyid[lanes, :] = jnp.broadcast_to(ids_row[:, lanes], (LANES, LANES)).T
            keylq[lanes, :] = jnp.broadcast_to(lq_row[:, lanes], (LANES, LANES)).T

    stats[0] = jnp.full((8, q_dev), LOW, jnp.float32)
    stats[1] = jnp.zeros((8, q_dev), jnp.float32)
    stats[2] = jnp.zeros((8, q_dev), jnp.float32)
    spread(0)

    def y_row(base, j):
        return lax.rem(base + n_rows - 2 * j, n_rows)

    aux_copies = []
    for s in range(1, n_rows):
        target = y_row(sib if s % 2 else row, s // 2)
        aux_copies.append(
            pltpu.make_async_remote_copy(
                src_ref=aux.at[0], dst_ref=aux.at[s], send_sem=aux_send.at[s],
                recv_sem=aux_recv.at[s], device_id=(target, col), device_id_type=MESH,
            )
        )
    def id_copy(k):
        to = lax.rem(me + k, n_dev)
        return pltpu.make_async_remote_copy(
            src_ref=idsend.at[lax.div(to, pack)],
            dst_ref=idrecv.at[lax.div(me, pack), lax.rem(me, pack)],
            send_sem=id_send.at[k], recv_sem=id_recv.at[k],
            device_id=place(to), device_id_type=MESH,
        )

    def own_emb_copy(s, i):
        target = sib if s == 1 else y_row(row, s // 2)
        return pltpu.make_async_remote_copy(
            src_ref=emb.at[0, i], dst_ref=emb.at[s, i], send_sem=emb_send.at[s, i],
            recv_sem=emb_recv.at[s, i], device_id=(target, col), device_id_type=MESH,
        )

    def fwd_copy(s, i):
        return pltpu.make_async_remote_copy(
            src_ref=emb.at[s, i], dst_ref=emb.at[s + 1, i], send_sem=fwd_send.at[s, i],
            recv_sem=fwd_recv.at[s, i], device_id=(sib, col), device_id_type=MESH,
        )

    direct = [1] + [2 * j for j in range(1, n_y)]
    loads[0].wait()
    loads[1].wait()

    def tower(i):
        feat_copy(i).wait()
        hidden = jnp.maximum(
            jnp.dot(feat[i], w_in[...], preferred_element_type=jnp.float32), 0.0
        ).astype(jnp.bfloat16)
        emb[0, i] = jnp.dot(hidden, w_out[...], preferred_element_type=jnp.float32).astype(
            jnp.bfloat16
        )

    def share(i):
        for s in reversed(direct):
            own_emb_copy(s, i).start()

    head = chunks // 2

    @pl.loop(0, head)
    def _(i):
        tower(i)

    pl.semaphore_wait(barrier, n_dev - 1)

    @pl.loop(0, head)
    def _(i):
        share(i)

    for copy in aux_copies:
        copy.start()

    @pl.loop(head, chunks)
    def _(i):
        tower(i)
        share(i)

    def a2a_copy(k):
        to = lax.rem(me + k, n_dev)
        return pltpu.make_async_remote_copy(
            src_ref=send.at[to], dst_ref=cache_ref.at[me],
            send_sem=a2a_send.at[k], recv_sem=a2a_recv.at[k],
            device_id=place(to), device_id_type=MESH,
        )

    own_block = pltpu.make_async_copy(send.at[me], cache_ref.at[me], own_sem)
    each = piece // cap
    groups = slots // piece
    first = lax.div(me, each) + 1

    @pl.loop(0, groups)
    def _(step):
        g = lax.rem(first + step, groups)
        hot = (
            lax.broadcasted_iota(jnp.int32, (piece, items), 0) + g * piece == slot
        ).astype(jnp.float32).astype(jnp.bfloat16)
        total = jnp.zeros((piece, width), jnp.float32)
        for i in range(chunks):
            total = total + jnp.dot(
                hot[:, i * chunk : (i + 1) * chunk], emb[0, i], preferred_element_type=jnp.float32
            )
        rows_out = total.astype(jnp.bfloat16)
        for t in range(each):
            send[g * each + t] = rows_out[t * cap : (t + 1) * cap, :]
        found = lax.dot_general(digits, hot, NT, preferred_element_type=jnp.float32)
        joined = jnp.sum(found.astype(jnp.int32) * weight, axis=0, keepdims=True) - 1
        for i in range(piece // LANES):
            idsend[g * (piece // LANES) + i] = joined[:, i * LANES : (i + 1) * LANES]

        @pl.loop(0, each)
        def _(t):
            k = lax.rem(g * each + t + n_dev - me, n_dev)

            @pl.when(k > 0)
            def _():
                a2a_copy(k).start()

    own_block.start()

    @pl.loop(1, n_dev)
    def _(k):
        id_copy(k).start()

    loads[2].wait()

    steep = 4.0 / math.sqrt(width) * math.log2(math.e)

    def score(s, i):
        @pl.loop(0, chunk // key_tile)
        def _(t):
            base = i * chunk + t * key_tile
            keys = emb[s, i, pl.ds(t * key_tile, key_tile), :]
            wide = query_tile // LANES
            ident = jnp.concatenate([keyid[pl.ds(base, key_tile), :]] * wide, axis=1)
            lq = jnp.concatenate([keylq[pl.ds(base, key_tile), :]] * wide, axis=1)
            ident = ident.reshape(key_tile // 8, 8, query_tile)
            for u in range(q_dev // query_tile):
                lanes = slice(u * query_tile, (u + 1) * query_tile)
                raw = lax.dot_general(keys, q[lanes, :], NT, preferred_element_type=jnp.float32) - lq
                raw = raw.reshape(key_tile // 8, 8, query_tile)
                hit = jnp.sum(jnp.where(ident == pos[:, lanes][None], raw, 0.0), axis=0)
                old = stats[0, :, lanes]
                top = jnp.maximum(old, jnp.max(raw, axis=0))
                total = jnp.sum(jnp.exp2((raw - top[None]) * steep), axis=0)
                stats[0, :, lanes] = top
                stats[1, :, lanes] = stats[1, :, lanes] * jnp.exp2((old - top) * steep) + total
                stats[2, :, lanes] = stats[2, :, lanes] + hit

    @pl.loop(0, chunks)
    def _(i):
        score(0, i)

    for s in range(1, n_rows):
        aux_copies[s - 1].wait()
        spread(s)

        @pl.loop(0, chunks)
        def _(i, s=s):
            if s == 1:
                own_emb_copy(1, i).wait()
            elif s % 2 == 0:
                own_emb_copy(s, i).wait()
                fwd_copy(s, i).start()
            else:
                fwd_copy(s - 1, i).wait()
            score(s, i)

    scale = 4.0 / math.sqrt(width)
    best = jnp.max(stats[0], axis=0, keepdims=True)
    mass = jnp.sum(stats[1] * jnp.exp2((stats[0] - best) * steep), axis=0, keepdims=True)
    parts[0, 0:1, :] = best * scale + jnp.log(mass)
    parts[0, 1:2, :] = jnp.sum(stats[2], axis=0, keepdims=True) * scale

    def stat_copy(k):
        return pltpu.make_async_remote_copy(
            src_ref=parts.at[0], dst_ref=parts.at[k],
            send_sem=stat_send.at[k], recv_sem=stat_recv.at[k],
            device_id=(row, lax.rem(col + k, n_cols)), device_id_type=MESH,
        )

    @pl.loop(1, n_cols)
    def _(k):
        stat_copy(k).start()

    idrecv[lax.div(me, pack), lax.rem(me, pack)] = idsend[lax.div(me, pack)]

    @pl.loop(1, n_dev)
    def _(k):
        id_copy(k).wait()

    lane = lax.broadcasted_iota(jnp.int32, (n_dev // pack, LANES), 1)
    result = jnp.zeros((n_dev // pack, LANES), jnp.int32)
    for j in range(pack):
        shift = lax.rem(j + pack - lax.rem(me, pack), pack) * cap
        for g in range(n_dev // pack):
            picked[g : g + 1, :] = idrecv[g, j, 0:1, :]
        turned = pltpu.roll(picked[...], shift, 1)
        result = jnp.where(lax.div(lane, cap) == j, turned, result)
    cids_ref[...] = result

    @pl.loop(1, n_cols)
    def _(k):
        stat_copy(k).wait()

    highest = parts[0, 0:1, :]
    for k in range(1, n_cols):
        highest = jnp.maximum(highest, parts[k, 0:1, :])
    summed = jnp.zeros_like(highest)
    positive = jnp.zeros_like(highest)
    for k in range(n_cols):
        summed = summed + jnp.exp(parts[k, 0:1, :] - highest)
        positive = positive + parts[k, 1:2, :]
    loss = highest + jnp.log(summed) - positive
    for i in range(q_dev // LANES):
        loss_ref[i : i + 1, :] = loss[:, i * LANES : (i + 1) * LANES]

    @pl.loop(1, n_dev)
    def _(k):
        a2a_copy(k).wait()

    own_block.wait()


def settle(*refs):
    sources, targets, held, sems = refs[0:3], refs[3:6], refs[6:9], refs[9]
    inward = [
        pltpu.make_async_copy(a, h, sems.at[i]) for i, (a, h) in enumerate(zip(sources, held))
    ]
    outward = [
        pltpu.make_async_copy(h, b, sems.at[3 + i]) for i, (h, b) in enumerate(zip(held, targets))
    ]
    for copy in inward:
        copy.start()
    for copy, onward in zip(inward[::-1], outward[::-1]):
        copy.wait()
        onward.start()
    for onward in outward:
        onward.wait()


def local(n_rows, n_cols, features, w_in, w_out, item_ids, item_counts, owners, queries, positives):
    n_dev = n_rows * n_cols
    items, wide = features.shape
    hid, width = w_out.shape
    cap = 2 * items // n_dev
    slots = n_dev * cap
    pack = LANES // cap
    q_dev = queries.shape[0]
    chunks = 4
    piece = 256
    bf16, i32, f32 = jnp.bfloat16, jnp.int32, jnp.float32
    hbm = pl.BlockSpec(memory_space=pl.ANY)
    vmem = pl.BlockSpec(memory_space=pltpu.VMEM)
    dma = pltpu.SemaphoreType.DMA
    cache, ids, loss = pl.pallas_call(
        functools.partial(kernel, n_rows, n_cols, cap, chunks, piece, 256, 512),
        out_shape=(
            jax.ShapeDtypeStruct((n_dev, cap, width), bf16),
            jax.ShapeDtypeStruct((slots // LANES, LANES), i32),
            jax.ShapeDtypeStruct((q_dev // LANES, LANES), f32),
        ),
        in_specs=[hbm, hbm, hbm, vmem, vmem, vmem, hbm, vmem],
        out_specs=(hbm, vmem, vmem),
        scratch_shapes=[
            pltpu.VMEM((chunks, items // chunks, wide), bf16),
            pltpu.VMEM(w_in.shape, bf16),
            pltpu.VMEM(w_out.shape, bf16),
            pltpu.VMEM(queries.shape, bf16),
            pltpu.VMEM((n_rows, chunks, items // chunks, width), bf16),
            pltpu.VMEM((n_rows, 8, items), i32),
            pltpu.VMEM((items, LANES), i32),
            pltpu.VMEM((items, LANES), f32),
            pltpu.VMEM((n_dev, cap, width), bf16),
            pltpu.VMEM((slots // LANES, 1, LANES), i32),
            pltpu.VMEM((n_dev // pack, pack, 1, LANES), i32),
            pltpu.VMEM((8, q_dev), i32),
            pltpu.VMEM((3, 8, q_dev), f32),
            pltpu.VMEM((n_cols, 2, q_dev), f32),
            pltpu.VMEM((n_dev // pack, LANES), i32),
            dma((3,)), dma((chunks,)), dma,
            dma((n_rows,)), dma((n_rows,)),
            dma((n_dev,)), dma((n_dev,)),
            dma((n_rows, chunks)), dma((n_rows, chunks)),
            dma((n_rows, chunks)), dma((n_rows, chunks)),
            dma((n_dev,)), dma((n_dev,)),
            dma((n_cols,)), dma((n_cols,)),
        ],
        compiler_params=pltpu.CompilerParams(
            collective_id=0, has_side_effects=True, vmem_limit_bytes=56 * 1024 * 1024
        ),
        name="refresh",
    )(
        features.reshape(chunks, items // chunks, wide),
        w_in,
        w_out,
        item_ids.reshape(items // LANES, LANES),
        item_counts.reshape(items // LANES, LANES),
        owners.reshape(items // LANES, LANES),
        queries,
        positives.reshape(positives.shape[0] // LANES, LANES),
    )
    cache, ids, loss = pl.pallas_call(
        settle,
        out_shape=tuple(jax.ShapeDtypeStruct(x.shape, x.dtype) for x in (cache, ids, loss)),
        in_specs=[hbm] * 3,
        out_specs=(hbm,) * 3,
        scratch_shapes=[pltpu.VMEM(x.shape, x.dtype) for x in (cache, ids, loss)] + [dma((6,))],
        compiler_params=pltpu.CompilerParams(vmem_limit_bytes=60 * 1024 * 1024),
        name="settle",
    )(cache, ids, loss)
    return cache.reshape(slots, width), ids.reshape(slots), loss.reshape(q_dev)


def solution(mesh):
    placed = (
        P(("rows", "cols"), None),
        P(),
        P(),
        P(("rows", "cols")),
        P(("rows", "cols")),
        P(("rows", "cols"), None),
        P("rows", None),
        P(),
    )
    return jax.shard_map(
        functools.partial(local, mesh.shape["rows"], mesh.shape["cols"]),
        mesh=mesh,
        in_specs=placed,
        out_specs=(P(("rows", "cols"), None), P(("rows", "cols")), P("rows")),
        check_vma=False,
    )
```
